32 devices in a mesh: rows: 8 (over y, x, core), cols: 4 (over z).
Axes of the slice: x: 2, y: 2, z: 4, core: 2. Of those that a mesh axis runs over, the one named last changes fastest.
Arguments:
- panel: float32 [2048, 256], P(('rows', 'cols')), may hold values from -1 to 1, as said below
- trailing: float32 [2048, 2048], P('rows', 'cols'), may hold values from -6 to 6
Outputs:
- r_factor: float32 [256, 256], replicated
- coefficients: float32 [256, 2048], P(None, 'cols')
- updated: float32 [2048, 2048], P('rows', 'cols')
The draws below stay inside these ranges and needn't reach their ends.
Inputs may be any that keep to these rules, and one draw needn't show every extreme that they name: panel has full column rank and is well conditioned; rows and columns carry different scales.
All inputs are finite; a program needn't handle non-finite values.
Results may differ from the reference program's by a relative error of at most 0.0003.
Values sent between devices are 32-bit elements; how exact they have to be, the bound alone decides.
No kernel may reach another device: no remote copies, remote signals or barrier semaphores. Data moves between devices by JAX's collectives and lax.ppermute only.
A program may use at most 64 MiB of HBM per device.

```python
import jax
import jax.numpy as jnp
from jax import lax

PANEL = 256
TRAIL = 2048
ROWS = 2048


def draw_panel(key, part):
    key_base = jax.random.fold_in(key, 11)
    key_mix = jax.random.fold_in(key, 12)
    key_scale = jax.random.fold_in(key, 13)
    base = jnp.clip(jax.random.normal(key_base, (ROWS, PANEL), jnp.float32), -6.0, 6.0)
    row_ramp = 1.0 + 2.0 * jnp.arange(ROWS, dtype=jnp.float32) / ROWS
    base = base * row_ramp[:, None] / jnp.sqrt(jnp.float32(ROWS))
    mixing = jnp.eye(PANEL, dtype=jnp.float32) + jax.random.uniform(key_mix, (PANEL, PANEL), jnp.float32, -0.5, 0.5) / jnp.sqrt(jnp.float32(PANEL))
    col_scale = jnp.exp(jax.random.uniform(key_scale, (PANEL,), jnp.float32, 0.0, 1.3862944))
    mixed = jnp.dot(base, mixing, precision=lax.Precision.HIGHEST) * col_scale[None, :]
    return jnp.clip(mixed, -1.0, 1.0)


def block_scale(key, dims, split, low, high):
    gain, own = 1.0, jax.random.fold_in(key, 6)
    for dim, parts in split:
        heights = jnp.exp(jax.random.uniform(jax.random.fold_in(own, dim), (parts,), jnp.float32, low / len(split), high / len(split)))
        gain = gain * jnp.repeat(heights, dims[dim] // parts).reshape([-1 if axis == dim else 1 for axis in range(len(dims))])
    return gain


def bell_draw(stream_key, shape, deviation, bound, pieces=(), kind=jnp.bfloat16):
    factor_of = block_scale(stream_key, shape, pieces, -0.22, 0.18) if pieces else 1.0
    entries = jax.random.normal(stream_key, shape, jnp.float32) * deviation * factor_of
    return jnp.minimum(jnp.maximum(entries, -bound), bound).astype(kind)


def setup_inputs(seed: int = 0) -> dict:
    streams_of = jax.random.split(jax.random.key(seed), 3)
    return {
        "panel": draw_panel(jax.random.fold_in(streams_of[2], 71), 0),
        "trailing": bell_draw(streams_of[1], (ROWS, TRAIL), 1.0, 6.0, ((0, 8), (1, 4)), jnp.float32),
    }


def reference(panel, trailing):
    r_raw = jnp.linalg.qr(panel, mode='r')
    diag_vals = jnp.diagonal(r_raw)
    sign_fix = jnp.where(diag_vals < 0, -1.0, 1.0).astype(r_raw.dtype)
    r_factor = sign_fix[:, None] * r_raw
    q_basis = jax.scipy.linalg.solve_triangular(r_factor, panel.T, trans=1, lower=False).T
    coefficients = jnp.dot(q_basis.T, trailing, precision=lax.Precision.HIGHEST)
    updated = trailing - jnp.dot(q_basis, coefficients, precision=lax.Precision.HIGHEST)
    return (r_factor, coefficients, updated)
```

```python
import functools

import jax
import jax.numpy as jnp
from jax import lax
from jax.experimental import pallas as pl
from jax.experimental.pallas import tpu as pltpu
from jax.sharding import PartitionSpec as P

LANES, SUBLANES, BLOCK = 128, 8, 32


def split(x):
    high = x.astype(jnp.bfloat16)
    return high, (x - high.astype(jnp.float32)).astype(jnp.bfloat16)


def product(left, right, over_left, over_right):
    lh, ll = split(left)
    rh, rl = split(right)
    return lax.dot_general(
        jnp.concatenate([lh, lh, ll], axis=over_left),
        jnp.concatenate([rh, rl, rh], axis=over_right),
        (((over_left,), (over_right,)), ((), ())),
        preferred_element_type=jnp.float32,
    )


def call(body, outs, *args, scratch=(), name=None, in_specs=None, out_specs=None):
    shapes = [jax.ShapeDtypeStruct(s, jnp.float32) for s in outs]
    extra = {}
    if in_specs is not None:
        extra["in_specs"] = in_specs
    if out_specs is not None:
        extra["out_specs"] = out_specs
    return pl.pallas_call(body, out_shape=shapes, scratch_shapes=list(scratch), name=name, **extra)(*args)


def gram_kernel(*refs, count):
    pieces, (panel_ref, keep_ref, send_ref) = refs[:count], refs[count:]
    height, width = pieces[0].shape
    half = width // 2
    here = lax.axis_index("cols")
    for step in range(count):
        at = lax.rem(here - step + count, count)
        panel_ref[pl.ds(pl.multiple_of(at * height, height), height), :] = pieces[step][...]
    block = panel_ref[...]
    gram = product(block, block, 0, 0)
    row = lax.broadcasted_iota(jnp.int32, (half, half), 0)
    col = lax.broadcasted_iota(jnp.int32, (half, half), 1)
    first, cross, second = gram[:half, :half], gram[:half, half:], gram[half:, half:]
    square = jnp.where(row > col, first, second)
    spare = jnp.sum(jnp.where(row == col, first, 0.0), axis=0, keepdims=True)
    spare = jnp.broadcast_to(spare, (SUBLANES, half))
    even = lax.rem(lax.axis_index("rows"), 2) == 0

    @pl.when(even)
    def _():
        keep_ref[:half, :] = cross
        keep_ref[half:, :] = jnp.zeros((SUBLANES, half), jnp.float32)
        send_ref[:half, :] = square
        send_ref[half:, :] = spare

    @pl.when(jnp.logical_not(even))
    def _():
        send_ref[:half, :] = cross
        send_ref[half:, :] = jnp.zeros((SUBLANES, half), jnp.float32)
        keep_ref[:half, :] = square
        keep_ref[half:, :] = spare


def unpack(mine_ref, other_ref, m_ref):
    width = m_ref.shape[0]
    half = width // 2
    even = lax.rem(lax.axis_index("rows"), 2) == 0

    def place(cross_ref, square_ref):
        square = square_ref[:half, :]
        spare = square_ref[half : half + 1, :]
        row = lax.broadcasted_iota(jnp.int32, (half, half), 0)
        col = lax.broadcasted_iota(jnp.int32, (half, half), 1)
        turned = square.T
        m_ref[:half, :half] = jnp.where(row > col, square, jnp.where(row < col, turned, spare))
        m_ref[half:, half:] = jnp.where(row <= col, square, turned)
        m_ref[:half, half:] = cross_ref[:half, :]
        m_ref[half:, :half] = jnp.zeros((half, half), jnp.float32)

    pl.when(even)(functools.partial(place, mine_ref, other_ref))
    pl.when(jnp.logical_not(even))(functools.partial(place, other_ref, mine_ref))


def along_sublanes(x, r):
    return jnp.broadcast_to(x[r : r + 1, :], x.shape)


def along_lanes(x, c):
    return jnp.broadcast_to(x[:, c : c + 1], (x.shape[0], LANES))


def factor_rows(rows, unit, tile, lane0):
    groups, tiles = len(rows), len(rows[0])
    sub = lax.broadcasted_iota(jnp.int32, (SUBLANES, LANES), 0)
    for j in range(groups):
        own = rows[j] + [unit[j]]
        out = list(own)
        col = {
            g: [along_lanes(rows[g][tile], lane0 + SUBLANES * j + c) for c in range(SUBLANES)] for g in range(j, groups)
        }
        pivot = {(r, c): along_sublanes(col[j][c], r) for c in range(SUBLANES) for r in range(c, SUBLANES)}
        low, done = {}, []
        for i in range(SUBLANES):
            scale = lax.rsqrt(pivot[i, i])
            for r in range(i + 1, SUBLANES):
                low[r, i] = pivot[r, i] * scale
            for c in range(i + 1, SUBLANES):
                for r in range(c, SUBLANES):
                    pivot[r, c] = pivot[r, c] - low[r, i] * low[c, i]
            solved = []
            for t in range(tiles + 1):
                x = along_sublanes(own[t], i)
                for m in range(i):
                    x = x - low[i, m] * done[m][t]
                x = x * scale
                solved.append(x)
                out[t] = jnp.where(sub == i, x, out[t])
            done.append(solved)
            for g in range(j + 1, groups):
                x = col[g][i]
                for m in range(i):
                    x = x - col[g][m] * low[i, m]
                col[g][i] = x * scale
        rows[j], unit[j] = out[:tiles], out[tiles]
        for g in range(j + 1, groups):
            for i in range(SUBLANES):
                for t in range(tiles):
                    rows[g][t] = rows[g][t] - col[g][i] * done[i][t]
                unit[g] = unit[g] - col[g][i] * done[i][tiles]


def factor_block(m_ref, r_ref, w_ref, k):
    n = m_ref.shape[0]
    tiles, groups = n // LANES, BLOCK // SUBLANES
    sub = lax.broadcasted_iota(jnp.int32, (SUBLANES, LANES), 0)
    lane = lax.broadcasted_iota(jnp.int32, (SUBLANES, LANES), 1)
    zeros = jnp.zeros((SUBLANES, LANES), jnp.float32)
    base = k * BLOCK
    tile, lane0 = base // LANES, base % LANES
    at = lambda g, t: (slice(base + SUBLANES * g, base + SUBLANES * (g + 1)), slice(LANES * t, LANES * (t + 1)))
    rows = [[m_ref[at(g, t)] for t in range(tiles)] for g in range(groups)]
    unit = [jnp.where(lane == lane0 + SUBLANES * g + sub, 1.0, 0.0).astype(jnp.float32) for g in range(groups)]
    factor_rows(rows, unit, tile, lane0)
    inside = (lane >= lane0) & (lane < lane0 + BLOCK)
    both = [[jnp.where(inside, unit[g], rows[g][t]) if t == tile else rows[g][t] for t in range(tiles)] for g in range(groups)]
    for g in range(groups):
        for t in range(tiles):
            c, r = lane + LANES * t, sub + base + SUBLANES * g
            r_ref[at(g, t)] = zeros if t < tile else rows[g][t] if t > tile else jnp.where(c >= r, rows[g][t], 0.0)
            w_ref[at(g, t)] = zeros if t > tile else rows[g][t] if t < tile else jnp.where(c <= r, both[g][t], 0.0)
    below = base + BLOCK
    if below < n:
        t0 = below // LANES
        right = jnp.concatenate([jnp.concatenate(both[g], axis=1) for g in range(groups)], axis=0)
        left = jnp.concatenate([jnp.concatenate(rows[g][t0:], axis=1) for g in range(groups)], axis=0)
        change = product(left[:, below - LANES * t0 :], right, 0, 0)
        c = lax.broadcasted_iota(jnp.int32, (n - below, n), 1)
        old = m_ref[below:, :]
        m_ref[below:, :] = jnp.where((c >= base) & (c < below), 0.0, old) - change


def factor_first_kernel(mine_ref, other_ref, m_ref, r_ref, w_ref):
    unpack(mine_ref, other_ref, m_ref)
    for k in range(m_ref.shape[0] // BLOCK // 2):
        factor_block(m_ref, r_ref, w_ref, k)


def factor_second_kernel(m_ref, r0_ref, w0_ref, r_ref, w_ref, work_ref):
    n = m_ref.shape[0]
    half = n // 2
    work_ref[...] = m_ref[...]
    r_ref[:half, :] = r0_ref[:half, :]
    w_ref[:half, :] = w0_ref[:half, :]
    for k in range(n // BLOCK // 2, n // BLOCK):
        factor_block(work_ref, r_ref, w_ref, k)


def cross_kernel(panel_ref, trailing_ref, keep_ref, send_ref):
    half = trailing_ref.shape[1] // 2
    terms = product(panel_ref[...], trailing_ref[...], 0, 0)
    even = lax.rem(lax.axis_index("rows"), 2) == 0

    @pl.when(even)
    def _():
        keep_ref[...] = terms[:, :half]
        send_ref[...] = terms[:, half:]

    @pl.when(jnp.logical_not(even))
    def _():
        keep_ref[...] = terms[:, half:]
        send_ref[...] = terms[:, :half]


def finish_kernel(w_ref, mine_ref, other_ref, panel_ref, trailing_ref, coefficients_ref, updated_ref):
    inverse = w_ref[...]
    even = lax.rem(lax.axis_index("rows"), 2) == 0
    mine, other = mine_ref[...], other_ref[...]
    terms = jnp.concatenate([jnp.where(even, mine, other), jnp.where(even, other, mine)], axis=1)
    coefficients = product(inverse, terms, 1, 0)
    coefficients_ref[...] = coefficients
    basis = product(panel_ref[...], inverse, 1, 1)
    updated_ref[...] = trailing_ref[...] - product(basis, coefficients, 1, 0)


def local(panel, trailing, *, n_rows, n_cols):
    height, width = panel.shape
    tall, wide = trailing.shape
    half = width // 2
    bits = n_rows.bit_length() - 1
    links = bits - 1
    partner = [(i, i ^ 1) for i in range(n_rows)]
    rounds = []
    for t in range(links):
        bit = [1 + t, 1 + (t + links // 2) % links]
        rounds.append([(i, i ^ (1 << bit[i % 2])) for i in range(n_rows)])

    pieces = [panel]
    for step in range(1, n_cols):
        pieces.append(lax.ppermute(panel, "cols", [(i, (i + step) % n_cols) for i in range(n_cols)]))
    packed = (half + SUBLANES, half)
    panel_block, g, g_send = call(
        functools.partial(gram_kernel, count=n_cols), [(tall, width), packed, packed], *pieces, name="gram"
    )
    g = g + lax.ppermute(g_send, "rows", partner)
    c, c_send = call(cross_kernel, [(width, wide // 2)] * 2, panel_block, trailing, name="cross")
    c = c + lax.ppermute(c_send, "rows", partner)
    for pairs in rounds:
        g = g + lax.ppermute(g, "rows", pairs)
    for pairs in rounds:
        c = c + lax.ppermute(c, "rows", pairs)
    g_other = lax.ppermute(g, "rows", partner)
    c_other = lax.ppermute(c, "rows", partner)
    m, r, w = call(factor_first_kernel, [(width, width)] * 3, g, g_other, name="factor_first")
    r, w = call(
        factor_second_kernel,
        [(width, width)] * 2,
        m,
        r,
        w,
        scratch=[pltpu.VMEM((width, width), jnp.float32)],
        name="factor_second",
    )
    coefficients, updated = call(
        finish_kernel, [(width, wide), (tall, wide)], w, c, c_other, panel_block, trailing, name="finish"
    )
    return r, coefficients, updated


def solution(mesh):
    return jax.shard_map(
        functools.partial(local, n_rows=mesh.shape["rows"], n_cols=mesh.shape["cols"]),
        mesh=mesh,
        in_specs=(P(("rows", "cols"), None), P("rows", "cols")),
        out_specs=(P(), P(None, "cols"), P("rows", "cols")),
        check_vma=False,
    )
```

```python
import functools

import jax
import jax.numpy as jnp
from jax import lax
from jax.experimental import pallas as pl
from jax.experimental.pallas import tpu as pltpu
from jax.sharding import PartitionSpec as P


LANES, SUBLANES, BLOCK, PARTS = 128, 8, 32, 4


def split(x):
    high = x.astype(jnp.bfloat16)
    return high, (x - high.astype(jnp.float32)).astype(jnp.bfloat16)


def product(left, right, over_left, over_right):
    lh, ll = split(left)
    rh, rl = split(right)
    return lax.dot_general(
        jnp.concatenate([lh, lh, ll], axis=over_left),
        jnp.concatenate([rh, rl, rh], axis=over_right),
        (((over_left,), (over_right,)), ((), ())),
        preferred_element_type=jnp.float32,
    )


def call(body, outs, *args, aliases=None, in_vmem=True, **extra):
    block = pl.BlockSpec(memory_space=pltpu.VMEM)
    shapes = [(pltpu.VMEM if in_vmem else jax.ShapeDtypeStruct)(s, jnp.float32) for s in outs]
    args = [pltpu.with_memory_space_constraint(x, pltpu.VMEM) for x in args]
    extra = {"in_specs": [block] * len(args), "out_specs": [block] * len(outs)} | extra
    return pl.pallas_call(body, out_shape=shapes, input_output_aliases=aliases or {}, **extra)(*args)


def stage_kernel(panel_hbm, trailing_hbm, panel_ref, trailing_ref, sems):
    copies = [
        pltpu.make_async_copy(panel_hbm, panel_ref, sems.at[0]),
        pltpu.make_async_copy(trailing_hbm, trailing_ref, sems.at[1]),
    ]
    for copy in copies:
        copy.start()
    for copy in copies:
        copy.wait()


def gram_kernel(*refs, count):
    pieces, (panel_ref, keep_ref, send_ref) = refs[:count], refs[count:]
    height, width = pieces[0].shape
    half = width // 2
    here = lax.axis_index("cols")
    for step in range(count):
        at = lax.rem(here - step + count, count)
        panel_ref[pl.ds(pl.multiple_of(at * height, height), height), :] = pieces[step][...]
    block = panel_ref[...]
    gram = product(block, block, 0, 0)
    row = lax.broadcasted_iota(jnp.int32, (half, half), 0)
    col = lax.broadcasted_iota(jnp.int32, (half, half), 1)
    first, cross, second = gram[:half, :half], gram[:half, half:], gram[half:, half:]
    square = jnp.where(row > col, first, second)
    spare = jnp.sum(jnp.where(row == col, first, 0.0), axis=0, keepdims=True)
    spare = jnp.broadcast_to(spare, (SUBLANES, half))
    even = lax.rem(lax.axis_index("rows"), 2) == 0

    @pl.when(even)
    def _():
        keep_ref[:half, :] = cross
        keep_ref[half:, :] = jnp.zeros((SUBLANES, half), jnp.float32)
        send_ref[:half, :] = square
        send_ref[half:, :] = spare

    @pl.when(jnp.logical_not(even))
    def _():
        send_ref[:half, :] = cross
        send_ref[half:, :] = jnp.zeros((SUBLANES, half), jnp.float32)
        keep_ref[:half, :] = square
        keep_ref[half:, :] = spare


def unpack(mine_ref, other_ref, m_ref):
    width = m_ref.shape[0]
    half = width // 2
    even = lax.rem(lax.axis_index("rows"), 2) == 0

    def place(cross_ref, square_ref):
        square = square_ref[:half, :]
        spare = square_ref[half : half + 1, :]
        row = lax.broadcasted_iota(jnp.int32, (half, half), 0)
        col = lax.broadcasted_iota(jnp.int32, (half, half), 1)
        turned = square.T
        m_ref[:half, :half] = jnp.where(row > col, square, jnp.where(row < col, turned, spare))
        m_ref[half:, half:] = jnp.where(row <= col, square, turned)
        m_ref[:half, half:] = cross_ref[:half, :]
        m_ref[half:, :half] = jnp.zeros((half, half), jnp.float32)

    pl.when(even)(functools.partial(place, mine_ref, other_ref))
    pl.when(jnp.logical_not(even))(functools.partial(place, other_ref, mine_ref))


def along_sublanes(x, r):
    return jnp.broadcast_to(x[r : r + 1, :], x.shape)


def along_lanes(x, c):
    return jnp.broadcast_to(x[:, c : c + 1], (x.shape[0], LANES))


def factor_rows(rows, unit, tile, lane0):
    groups, tiles = len(rows), len(rows[0])
    sub = lax.broadcasted_iota(jnp.int32, (SUBLANES, LANES), 0)
    for j in range(groups):
        own = rows[j] + [unit[j]]
        out = list(own)
        col = {
            g: [along_lanes(rows[g][tile], lane0 + SUBLANES * j + c) for c in range(SUBLANES)] for g in range(j, groups)
        }
        pivot = {(r, c): along_sublanes(col[j][c], r) for c in range(SUBLANES) for r in range(c, SUBLANES)}
        low, done = {}, []
        for i in range(SUBLANES):
            scale = lax.rsqrt(pivot[i, i])
            for r in range(i + 1, SUBLANES):
                low[r, i] = pivot[r, i] * scale
            for c in range(i + 1, SUBLANES):
                for r in range(c, SUBLANES):
                    pivot[r, c] = pivot[r, c] - low[r, i] * low[c, i]
            solved = []
            for t in range(tiles + 1):
                x = along_sublanes(own[t], i)
                for m in range(i):
                    x = x - low[i, m] * done[m][t]
                x = x * scale
                solved.append(x)
                out[t] = jnp.where(sub == i, x, out[t])
            done.append(solved)
            for g in range(j + 1, groups):
                x = col[g][i]
                for m in range(i):
                    x = x - col[g][m] * low[i, m]
                col[g][i] = x * scale
        rows[j], unit[j] = out[:tiles], out[tiles]
        for g in range(j + 1, groups):
            for i in range(SUBLANES):
                for t in range(tiles):
                    rows[g][t] = rows[g][t] - col[g][i] * done[i][t]
                unit[g] = unit[g] - col[g][i] * done[i][tiles]


def factor_block(m_ref, r_ref, w_ref, k):
    n = m_ref.shape[0]
    tiles, groups = n // LANES, BLOCK // SUBLANES
    sub = lax.broadcasted_iota(jnp.int32, (SUBLANES, LANES), 0)
    lane = lax.broadcasted_iota(jnp.int32, (SUBLANES, LANES), 1)
    zeros = jnp.zeros((SUBLANES, LANES), jnp.float32)
    base = k * BLOCK
    tile, lane0 = base // LANES, base % LANES
    at = lambda g, t: (slice(base + SUBLANES * g, base + SUBLANES * (g + 1)), slice(LANES * t, LANES * (t + 1)))
    rows = [[m_ref[at(g, t)] for t in range(tiles)] for g in range(groups)]
    unit = [jnp.where(lane == lane0 + SUBLANES * g + sub, 1.0, 0.0).astype(jnp.float32) for g in range(groups)]
    factor_rows(rows, unit, tile, lane0)
    inside = (lane >= lane0) & (lane < lane0 + BLOCK)
    both = [[jnp.where(inside, unit[g], rows[g][t]) if t == tile else rows[g][t] for t in range(tiles)] for g in range(groups)]
    for g in range(groups):
        for t in range(tiles):
            c, r = lane + LANES * t, sub + base + SUBLANES * g
            r_ref[at(g, t)] = zeros if t < tile else rows[g][t] if t > tile else jnp.where(c >= r, rows[g][t], 0.0)
            w_ref[at(g, t)] = zeros if t > tile else rows[g][t] if t < tile else jnp.where(c <= r, both[g][t], 0.0)
    below = base + BLOCK
    if below < n:
        t0 = below // LANES
        right = jnp.concatenate([jnp.concatenate(both[g], axis=1) for g in range(groups)], axis=0)
        left = jnp.concatenate([jnp.concatenate(rows[g][t0:], axis=1) for g in range(groups)], axis=0)
        change = product(left[:, below - LANES * t0 :], right, 0, 0)
        c = lax.broadcasted_iota(jnp.int32, (n - below, n), 1)
        old = m_ref[below:, :]
        m_ref[below:, :] = jnp.where((c >= base) & (c < below), 0.0, old) - change


def factor_first_kernel(mine_ref, other_ref, m_ref, r_ref, w_ref, *, stop):
    unpack(mine_ref, other_ref, m_ref)
    for k in range(stop):
        factor_block(m_ref, r_ref, w_ref, k)


def factor_more_kernel(m0_ref, r0_ref, w0_ref, m_ref, r_ref, w_ref, *, start, stop):
    for k in range(start, stop):
        factor_block(m_ref, r_ref, w_ref, k)


def cross_kernel(panel_ref, trailing_ref, keep_ref, send_ref):
    half = trailing_ref.shape[1] // 2
    terms = product(panel_ref[...], trailing_ref[...], 0, 0)
    even = lax.rem(lax.axis_index("rows"), 2) == 0

    @pl.when(even)
    def _():
        keep_ref[...] = terms[:, :half]
        send_ref[...] = terms[:, half:]

    @pl.when(jnp.logical_not(even))
    def _():
        keep_ref[...] = terms[:, half:]
        send_ref[...] = terms[:, :half]


def finish_kernel(w_ref, mine_ref, other_ref, panel_ref, trailing_ref, coefficients_ref, updated_ref, c_ref, u_ref, sems):
    inverse = w_ref[...]
    even = lax.rem(lax.axis_index("rows"), 2) == 0
    mine, other = mine_ref[...], other_ref[...]
    terms = jnp.concatenate([jnp.where(even, mine, other), jnp.where(even, other, mine)], axis=1)
    coefficients = product(inverse, terms, 1, 0)
    c_ref[...] = coefficients
    copies = [pltpu.make_async_copy(c_ref, coefficients_ref, sems.at[0])]
    copies[0].start()
    basis = product(panel_ref[...], inverse, 1, 1)
    tall = u_ref.shape[0] // PARTS
    for part in range(PARTS):
        at = slice(part * tall, (part + 1) * tall)
        u_ref[at, :] = trailing_ref[at, :] - product(basis[at, :], coefficients, 1, 0)
        copies.append(pltpu.make_async_copy(u_ref.at[at, :], updated_ref.at[at, :], sems.at[1 + part]))
        copies[-1].start()
    for copy in copies:
        copy.wait()


def local(panel, trailing, *, n_rows, n_cols):
    _, width = panel.shape
    tall, wide = trailing.shape
    half = width // 2
    bits = n_rows.bit_length() - 1
    links = bits - 1
    partner = [(i, i ^ 1) for i in range(n_rows)]
    rounds = []
    for t in range(links):
        bit = [1 + t, 1 + (t + links // 2) % links]
        rounds.append([(i, i ^ (1 << bit[i % 2])) for i in range(n_rows)])

    def sent(x, pairs, axis="rows"):
        return lax.ppermute(x, axis, pairs)

    def summed(x, pairs):
        y = sent(x, pairs)
        return x + y

    panel_here, trailing = pl.pallas_call(
        stage_kernel,
        out_shape=[pltpu.VMEM(x.shape, x.dtype) for x in (panel, trailing)],
        in_specs=[pl.BlockSpec(memory_space=pl.ANY)] * 2,
        out_specs=[pl.BlockSpec(memory_space=pltpu.VMEM)] * 2,
        scratch_shapes=[pltpu.SemaphoreType.DMA((2,))],
        name="stage",
    )(panel, trailing)
    pieces = [panel_here]
    for step in range(1, n_cols):
        pieces.append(sent(panel, [(i, (i + step) % n_cols) for i in range(n_cols)], "cols"))
    packed, square = (half + SUBLANES, half), (width, width)
    panel_block, g, g_send = call(
        functools.partial(gram_kernel, count=n_cols), [(tall, width), packed, packed], *pieces
    )
    g = g + sent(g_send, partner)
    c, c_send = call(cross_kernel, [(width, wide // 2)] * 2, panel_block, trailing)
    c_got = sent(c_send, partner)
    c = c + c_got
    for pairs in rounds:
        g = summed(g, pairs)
    g_other = sent(g, partner)
    for pairs in rounds[:-1]:
        c = summed(c, pairs)
    blocks = width // BLOCK
    cuts = [blocks * 3 // 8, blocks * 7 // 8, blocks]
    state = call(functools.partial(factor_first_kernel, stop=cuts[0]), [square] * 3, g, g_other)
    c = summed(c, rounds[-1])
    for i in (1, 2):
        state = call(
            functools.partial(factor_more_kernel, start=cuts[i - 1], stop=cuts[i]),
            [square] * 3,
            *state,
            aliases={0: 0, 1: 1, 2: 2},
        )
        if i == 1:
            c_other = sent(c, partner)
    _, r, w = state
    hbm = pl.BlockSpec(memory_space=pl.ANY)
    coefficients, updated = call(
        finish_kernel,
        [(width, wide), (tall, wide)],
        w,
        c,
        c_other,
        panel_block,
        trailing,
        in_vmem=False,
        out_specs=[hbm, hbm],
        scratch_shapes=[
            pltpu.VMEM((width, wide), jnp.float32),
            pltpu.VMEM((tall, wide), jnp.float32),
            pltpu.SemaphoreType.DMA((1 + PARTS,)),
        ],
    )
    return r, coefficients, updated


def solution(mesh):
    n_rows = mesh.shape["rows"]
    return jax.shard_map(
        functools.partial(local, n_rows=n_rows, n_cols=mesh.shape["cols"]),
        mesh=mesh,
        in_specs=(P(("rows", "cols"), None), P("rows", "cols")),
        out_specs=(P(), P(None, "cols"), P("rows", "cols")),
        check_vma=False,
    )
```

```python
import functools

import jax
import jax.numpy as jnp
from jax import lax
from jax.experimental import pallas as pl
from jax.experimental.pallas import tpu as pltpu
from jax.sharding import PartitionSpec as P


LANES, SUBLANES, BLOCK, PARTS = 128, 8, 32, 4


def split(x):
    high = x.astype(jnp.bfloat16)
    return high, (x - high.astype(jnp.float32)).astype(jnp.bfloat16)


def product(left, right, over_left, over_right):
    lh, ll = split(left)
    rh, rl = split(right)
    return lax.dot_general(
        jnp.concatenate([lh, lh, ll], axis=over_left),
        jnp.concatenate([rh, rl, rh], axis=over_right),
        (((over_left,), (over_right,)), ((), ())),
        preferred_element_type=jnp.float32,
    )


def call(body, outs, *args, aliases=None, in_vmem=True, **extra):
    block = pl.BlockSpec(memory_space=pltpu.VMEM)
    shapes = [(pltpu.VMEM if in_vmem else jax.ShapeDtypeStruct)(s, jnp.float32) for s in outs]
    args = [pltpu.with_memory_space_constraint(x, pltpu.VMEM) for x in args]
    extra = {"in_specs": [block] * len(args), "out_specs": [block] * len(outs)} | extra
    return pl.pallas_call(body, out_shape=shapes, input_output_aliases=aliases or {}, **extra)(*args)


def stage_kernel(panel_hbm, trailing_hbm, panel_ref, trailing_ref, sems):
    copies = [
        pltpu.make_async_copy(panel_hbm, panel_ref, sems.at[0]),
        pltpu.make_async_copy(trailing_hbm, trailing_ref, sems.at[1]),
    ]
    for copy in copies:
        copy.start()
    for copy in copies:
        copy.wait()


def gram_kernel(*refs, count):
    pieces, (panel_ref, keep_ref, send_ref) = refs[:count], refs[count:]
    height, width = pieces[0].shape
    half = width // 2
    here = lax.axis_index("cols")
    for step in range(count):
        at = here ^ step
        panel_ref[pl.ds(pl.multiple_of(at * height, height), height), :] = pieces[step][...]
    block = panel_ref[...]
    gram = product(block, block, 0, 0)
    row = lax.broadcasted_iota(jnp.int32, (half, half), 0)
    col = lax.broadcasted_iota(jnp.int32, (half, half), 1)
    first, cross, second = gram[:half, :half], gram[:half, half:], gram[half:, half:]
    square = jnp.where(row > col, first, second)
    spare = jnp.sum(jnp.where(row == col, first, 0.0), axis=0, keepdims=True)
    spare = jnp.broadcast_to(spare, (SUBLANES, half))
    even = lax.rem(lax.axis_index("rows"), 2) == 0

    @pl.when(even)
    def _():
        keep_ref[:half, :] = cross
        keep_ref[half:, :] = jnp.zeros((SUBLANES, half), jnp.float32)
        send_ref[:half, :] = square
        send_ref[half:, :] = spare

    @pl.when(jnp.logical_not(even))
    def _():
        send_ref[:half, :] = cross
        send_ref[half:, :] = jnp.zeros((SUBLANES, half), jnp.float32)
        keep_ref[:half, :] = square
        keep_ref[half:, :] = spare


def unpack(mine_ref, other_ref, m_ref):
    width = m_ref.shape[0]
    half = width // 2
    even = lax.rem(lax.axis_index("rows"), 2) == 0

    def place(cross_ref, square_ref):
        square = square_ref[:half, :]
        spare = square_ref[half : half + 1, :]
        row = lax.broadcasted_iota(jnp.int32, (half, half), 0)
        col = lax.broadcasted_iota(jnp.int32, (half, half), 1)
        turned = square.T
        m_ref[:half, :half] = jnp.where(row > col, square, jnp.where(row < col, turned, spare))
        m_ref[half:, half:] = jnp.where(row <= col, square, turned)
        m_ref[:half, half:] = cross_ref[:half, :]
        m_ref[half:, :half] = jnp.zeros((half, half), jnp.float32)

    pl.when(even)(functools.partial(place, mine_ref, other_ref))
    pl.when(jnp.logical_not(even))(functools.partial(place, other_ref, mine_ref))


def along_sublanes(x, r):
    return jnp.broadcast_to(x[r : r + 1, :], x.shape)


def along_lanes(x, c):
    return jnp.broadcast_to(x[:, c : c + 1], (x.shape[0], LANES))


def factor_rows(rows, unit, tile, lane0, zero):
    groups, tiles = len(rows), len(rows[0])
    sub = lax.broadcasted_iota(jnp.int32, (SUBLANES, LANES), 0)
    for j in range(groups):
        own = rows[j] + [unit[j]]
        col = {
            g: [along_lanes(rows[g][tile], lane0 + SUBLANES * j + c) for c in range(SUBLANES)] for g in range(j, groups)
        }
        head = [x - zero for x in col[j]]
        pivot = {(r, c): along_sublanes(head[c], r) for c in range(SUBLANES) for r in range(c, SUBLANES)}
        low, done, scales = {}, [], zero
        for i in range(SUBLANES):
            scale = lax.rsqrt(pivot[i, i])
            scales = jnp.where(sub == i, scale, scales)
            below = zero
            for r in range(i + 1, SUBLANES):
                low[r, i] = pivot[r, i] * scale
                below = jnp.where(sub == r, low[r, i], below)
            for c in range(i + 1, SUBLANES):
                for r in range(c, SUBLANES):
                    pivot[r, c] = pivot[r, c] - low[r, i] * low[c, i]
            done.append([along_sublanes(x, i) * scale for x in own])
            if i + 1 < SUBLANES:
                own = [x - below * y for x, y in zip(own, done[i])]
            for g in range(j + 1, groups):
                x = col[g][i]
                for m in range(i):
                    x = x - col[g][m] * low[i, m]
                col[g][i] = x * scale
        own = [x * scales for x in own]
        rows[j], unit[j] = own[:tiles], own[tiles]
        for g in range(j + 1, groups):
            for i in range(SUBLANES):
                for t in range(tiles):
                    rows[g][t] = rows[g][t] - col[g][i] * done[i][t]
                unit[g] = unit[g] - col[g][i] * done[i][tiles]


def factor_block(m_ref, r_ref, w_ref, zero_ref, k):
    n = m_ref.shape[0]
    tiles, groups = n // LANES, BLOCK // SUBLANES
    sub = lax.broadcasted_iota(jnp.int32, (SUBLANES, LANES), 0)
    lane = lax.broadcasted_iota(jnp.int32, (SUBLANES, LANES), 1)
    zeros = jnp.zeros((SUBLANES, LANES), jnp.float32)
    base = k * BLOCK
    tile, lane0 = base // LANES, base % LANES
    at = lambda g, t: (slice(base + SUBLANES * g, base + SUBLANES * (g + 1)), slice(LANES * t, LANES * (t + 1)))
    rows = [[m_ref[at(g, t)] for t in range(tiles)] for g in range(groups)]
    unit = [jnp.where(lane == lane0 + SUBLANES * g + sub, 1.0, 0.0).astype(jnp.float32) for g in range(groups)]
    factor_rows(rows, unit, tile, lane0, zero_ref[...])
    inside = (lane >= lane0) & (lane < lane0 + BLOCK)
    both = [[jnp.where(inside, unit[g], rows[g][t]) if t == tile else rows[g][t] for t in range(tiles)] for g in range(groups)]
    for g in range(groups):
        for t in range(tiles):
            c, r = lane + LANES * t, sub + base + SUBLANES * g
            r_ref[at(g, t)] = zeros if t < tile else rows[g][t] if t > tile else jnp.where(c >= r, rows[g][t], 0.0)
            w_ref[at(g, t)] = zeros if t > tile else rows[g][t] if t < tile else jnp.where(c <= r, both[g][t], 0.0)
    below = base + BLOCK
    if below < n:
        t0 = below // LANES
        right = jnp.concatenate([jnp.concatenate(both[g], axis=1) for g in range(groups)], axis=0)
        left = jnp.concatenate([jnp.concatenate(rows[g][t0:], axis=1) for g in range(groups)], axis=0)
        change = product(left[:, below - LANES * t0 :], right, 0, 0)
        c = lax.broadcasted_iota(jnp.int32, (n - below, n), 1)
        old = m_ref[below:, :]
        m_ref[below:, :] = jnp.where((c >= base) & (c < below), 0.0, old) - change


def factor_first_kernel(mine_ref, other_ref, m_ref, r_ref, w_ref, zero_ref, *, stop):
    zero_ref[...] = jnp.zeros_like(zero_ref)
    unpack(mine_ref, other_ref, m_ref)
    for k in range(stop):
        factor_block(m_ref, r_ref, w_ref, zero_ref, k)


def factor_more_kernel(m0_ref, r0_ref, w0_ref, m_ref, r_ref, w_ref, zero_ref, *, start, stop):
    zero_ref[...] = jnp.zeros_like(zero_ref)
    for k in range(start, stop):
        factor_block(m_ref, r_ref, w_ref, zero_ref, k)


def cross_kernel(panel_ref, trailing_ref, keep_ref, send_ref):
    half = trailing_ref.shape[1] // 2
    terms = product(panel_ref[...], trailing_ref[...], 0, 0)
    even = lax.rem(lax.axis_index("rows"), 2) == 0

    @pl.when(even)
    def _():
        keep_ref[...] = terms[:, :half]
        send_ref[...] = terms[:, half:]

    @pl.when(jnp.logical_not(even))
    def _():
        keep_ref[...] = terms[:, half:]
        send_ref[...] = terms[:, :half]


def finish_kernel(
    r_ref, w_ref, mine_ref, other_ref, panel_ref, trailing_ref, factor_ref, coefficients_ref, updated_ref, c_ref, u_ref, sems
):
    copies = [pltpu.make_async_copy(r_ref, factor_ref, sems.at[1 + PARTS])]
    copies[0].start()
    inverse = w_ref[...]
    even = lax.rem(lax.axis_index("rows"), 2) == 0
    mine, other = mine_ref[...], other_ref[...]
    terms = jnp.concatenate([jnp.where(even, mine, other), jnp.where(even, other, mine)], axis=1)
    coefficients = product(inverse, terms, 1, 0)
    c_ref[...] = coefficients
    copies.append(pltpu.make_async_copy(c_ref, coefficients_ref, sems.at[0]))
    copies[-1].start()
    basis = product(panel_ref[...], inverse, 1, 1)
    tall = u_ref.shape[0] // PARTS
    for part in range(PARTS):
        at = slice(part * tall, (part + 1) * tall)
        u_ref[at, :] = trailing_ref[at, :] - product(basis[at, :], coefficients, 1, 0)
        copies.append(pltpu.make_async_copy(u_ref.at[at, :], updated_ref.at[at, :], sems.at[1 + part]))
        copies[-1].start()
    for copy in copies:
        copy.wait()


def gather_steps(n_cols):
    return [*range(n_cols // 2, n_cols), *range(1, n_cols // 2)]


def local(panel, trailing, *, n_rows, n_cols):
    _, width = panel.shape
    tall, wide = trailing.shape
    half = width // 2
    bits = n_rows.bit_length() - 1
    links = bits - 1
    partner = [(i, i ^ 1) for i in range(n_rows)]
    rounds = []
    for t in range(links):
        bit = [1 + t, 1 + (t + links // 2) % links]
        rounds.append([(i, i ^ (1 << bit[i % 2])) for i in range(n_rows)])

    def sent(x, pairs, axis="rows"):
        return lax.ppermute(x, axis, pairs)

    def summed(x, pairs):
        y = sent(x, pairs)
        return x + y

    panel_here, trailing = pl.pallas_call(
        stage_kernel,
        out_shape=[pltpu.VMEM(x.shape, x.dtype) for x in (panel, trailing)],
        in_specs=[pl.BlockSpec(memory_space=pl.ANY)] * 2,
        out_specs=[pl.BlockSpec(memory_space=pltpu.VMEM)] * 2,
        scratch_shapes=[pltpu.SemaphoreType.DMA((2,))],
        name="stage",
    )(panel, trailing)
    pieces = [panel_here]
    steps = gather_steps(n_cols)
    got = {step: sent(panel, [(i, i ^ step) for i in range(n_cols)], "cols") for step in steps}
    pieces += [got[step] for step in range(1, n_cols)]
    packed, square = (half + SUBLANES, half), (width, width)
    panel_block, g, g_send = call(
        functools.partial(gram_kernel, count=n_cols), [(tall, width), packed, packed], *pieces
    )
    g = g + sent(g_send, partner)
    c, c_send = call(cross_kernel, [(width, wide // 2)] * 2, panel_block, trailing)
    c_got = sent(c_send, partner)
    c = c + c_got
    for pairs in rounds:
        g = summed(g, pairs)
    g_other = sent(g, partner)
    for pairs in rounds:
        c = summed(c, pairs)
    blocks = width // BLOCK
    zero = [pltpu.VMEM((SUBLANES, LANES), jnp.float32)]
    cuts = [blocks * 7 // 8, blocks]
    state = call(functools.partial(factor_first_kernel, stop=cuts[0]), [square] * 3, g, g_other, scratch_shapes=zero)
    c_other = sent(c, partner)
    for i in (1,):
        state = call(
            functools.partial(factor_more_kernel, start=cuts[i - 1], stop=cuts[i]),
            [square] * 3,
            *state,
            scratch_shapes=zero,
            aliases={0: 0, 1: 1, 2: 2},
        )
    _, r, w = state
    hbm = pl.BlockSpec(memory_space=pl.ANY)
    return call(
        finish_kernel,
        [square, (width, wide), (tall, wide)],
        r,
        w,
        c,
        c_other,
        panel_block,
        trailing,
        in_vmem=False,
        out_specs=[hbm] * 3,
        scratch_shapes=[
            pltpu.VMEM((width, wide), jnp.float32),
            pltpu.VMEM((tall, wide), jnp.float32),
            pltpu.SemaphoreType.DMA((2 + PARTS,)),
        ],
    )


def solution(mesh):
    n_rows, n_cols = mesh.shape["rows"], mesh.shape["cols"]
    return jax.shard_map(
        functools.partial(local, n_rows=n_rows, n_cols=n_cols),
        mesh=mesh,
        in_specs=(P(("rows", "cols"), None), P("rows", "cols")),
        out_specs=(P(), P(None, "cols"), P("rows", "cols")),
        check_vma=False,
    )
```

```python
import functools

import jax
import jax.numpy as jnp
from jax import lax
from jax.experimental import pallas as pl
from jax.experimental.pallas import tpu as pltpu
from jax.sharding import PartitionSpec as P


LANES, SUBLANES, BLOCK, INNER, PARTS = 128, 8, 32, 4, 4

SMALL = pltpu.CompilerParams(vmem_limit_bytes=16 << 20)


def split(x):
    high = x.astype(jnp.bfloat16)
    return high, (x - high.astype(jnp.float32)).astype(jnp.bfloat16)


def product(left, right, over_left, over_right):
    lh, ll = split(left)
    rh, rl = split(right)
    return lax.dot_general(
        jnp.concatenate([lh, lh, ll], axis=over_left),
        jnp.concatenate([rh, rl, rh], axis=over_right),
        (((over_left,), (over_right,)), ((), ())),
        preferred_element_type=jnp.float32,
    )


def call(body, outs, *args, aliases=None, in_vmem=True, **extra):
    block = pl.BlockSpec(memory_space=pltpu.VMEM)
    shapes = [(pltpu.VMEM if in_vmem else jax.ShapeDtypeStruct)(s, jnp.float32) for s in outs]
    args = [pltpu.with_memory_space_constraint(x, pltpu.VMEM) for x in args]
    extra = {"in_specs": [block] * len(args), "out_specs": [block] * len(outs), "compiler_params": SMALL} | extra
    return pl.pallas_call(body, out_shape=shapes, input_output_aliases=aliases or {}, **extra)(*args)


def stage_kernel(panel_hbm, trailing_hbm, panel_ref, trailing_ref, sems):
    copies = [
        pltpu.make_async_copy(panel_hbm, panel_ref, sems.at[0]),
        pltpu.make_async_copy(trailing_hbm, trailing_ref, sems.at[1]),
    ]
    for copy in copies:
        copy.start()
    for copy in copies:
        copy.wait()


def gram_kernel(*refs, count):
    pieces, (panel_ref, keep_ref, send_ref) = refs[:count], refs[count:]
    height, width = pieces[0].shape
    half = width // 2
    here = lax.axis_index("cols")
    for step in range(count):
        at = here ^ step
        panel_ref[pl.ds(pl.multiple_of(at * height, height), height), :] = pieces[step][...]
    block = panel_ref[...]
    gram = product(block, block, 0, 0)
    row = lax.broadcasted_iota(jnp.int32, (half, half), 0)
    col = lax.broadcasted_iota(jnp.int32, (half, half), 1)
    first, cross, second = gram[:half, :half], gram[:half, half:], gram[half:, half:]
    square = jnp.where(row > col, first, second)
    spare = jnp.sum(jnp.where(row == col, first, 0.0), axis=0, keepdims=True)
    spare = jnp.broadcast_to(spare, (SUBLANES, half))
    even = lax.rem(lax.axis_index("rows"), 2) == 0

    @pl.when(even)
    def _():
        keep_ref[:half, :] = cross
        keep_ref[half:, :] = jnp.zeros((SUBLANES, half), jnp.float32)
        send_ref[:half, :] = square
        send_ref[half:, :] = spare

    @pl.when(jnp.logical_not(even))
    def _():
        send_ref[:half, :] = cross
        send_ref[half:, :] = jnp.zeros((SUBLANES, half), jnp.float32)
        keep_ref[:half, :] = square
        keep_ref[half:, :] = spare


def unpack(mine_ref, other_ref, m_ref):
    width = m_ref.shape[0]
    half = width // 2
    even = lax.rem(lax.axis_index("rows"), 2) == 0

    def place(cross_ref, square_ref):
        square = square_ref[:half, :]
        spare = square_ref[half : half + 1, :]
        row = lax.broadcasted_iota(jnp.int32, (half, half), 0)
        col = lax.broadcasted_iota(jnp.int32, (half, half), 1)
        turned = square.T
        m_ref[:half, :half] = jnp.where(row > col, square, jnp.where(row < col, turned, spare))
        m_ref[half:, half:] = jnp.where(row <= col, square, turned)
        m_ref[:half, half:] = cross_ref[:half, :]
        m_ref[half:, :half] = jnp.zeros((half, half), jnp.float32)

    pl.when(even)(functools.partial(place, mine_ref, other_ref))
    pl.when(jnp.logical_not(even))(functools.partial(place, other_ref, mine_ref))


def along_sublanes(x, r):
    return jnp.broadcast_to(x[r : r + 1, :], x.shape)


def along_lanes(x, c):
    return jnp.broadcast_to(x[:, c : c + 1], (x.shape[0], LANES))


def factor_rows(rows, unit, tile, lane0, zero):
    groups, tiles = len(rows), len(rows[0])
    sub = lax.broadcasted_iota(jnp.int32, (SUBLANES, LANES), 0)
    for j in range(groups):
        own = rows[j] + [unit[j]]
        spread = lambda step: {
            g: [along_lanes(rows[g][tile], lane0 + SUBLANES * step + c) for c in range(SUBLANES)]
            for g in range(step, groups)
        }
        if j == 0:
            col = spread(0)
            col[0] = [x - zero for x in col[0]]
        else:
            col = following
        following = spread(j + 1)
        head = list(col[j])
        low, ours, done, scales = {}, [], [], zero
        for i in range(SUBLANES):
            start = i - i % INNER
            stop = start + INNER
            if i == start:
                for c in range(i, SUBLANES):
                    for m in range(max(start - INNER, 0), start):
                        low[c, m] = along_sublanes(ours[m], c)
                        head[c] = head[c] - ours[m] * low[c, m]
                pivot = {(r, c): along_sublanes(head[c], r) for c in range(i, stop) for r in range(c, stop)}
            scale = lax.rsqrt(pivot[i, i])
            scales = jnp.where(sub == i, scale, scales)
            for r in range(i + 1, stop):
                low[r, i] = pivot[r, i] * scale
            for c in range(i + 1, stop):
                for r in range(c, stop):
                    pivot[r, c] = pivot[r, c] - low[r, i] * low[c, i]
            x = head[i]
            for m in range(start, i):
                x = x - ours[m] * low[i, m]
            ours.append(x * scale)
            done.append([along_sublanes(x, i) * scale for x in own])
            if i + 1 < SUBLANES:
                below = jnp.where(sub > i, ours[i], zero)
                own = [x - below * y for x, y in zip(own, done[i])]
            for g in range(j + 1, groups):
                x = col[g][i]
                for m in range(i):
                    x = x - col[g][m] * low[i, m]
                col[g][i] = x * scale
            for c in range(SUBLANES if j + 1 < groups else 0):
                factor = along_sublanes(col[j + 1][i], c)
                for g in range(j + 1, groups):
                    following[g][c] = following[g][c] - col[g][i] * factor
        own = [x * scales for x in own]
        rows[j], unit[j] = own[:tiles], own[tiles]
        for g in range(j + 1, groups):
            for i in range(SUBLANES):
                for t in range(tiles):
                    rows[g][t] = rows[g][t] - col[g][i] * done[i][t]
                unit[g] = unit[g] - col[g][i] * done[i][tiles]


def factor_block(m_ref, r_ref, w_ref, zero_ref, k):
    n = m_ref.shape[0]
    tiles, groups = n // LANES, BLOCK // SUBLANES
    sub = lax.broadcasted_iota(jnp.int32, (SUBLANES, LANES), 0)
    lane = lax.broadcasted_iota(jnp.int32, (SUBLANES, LANES), 1)
    zeros = jnp.zeros((SUBLANES, LANES), jnp.float32)
    base = k * BLOCK
    tile, lane0 = base // LANES, base % LANES
    at = lambda g, t: (slice(base + SUBLANES * g, base + SUBLANES * (g + 1)), slice(LANES * t, LANES * (t + 1)))
    rows = [[m_ref[at(g, t)] for t in range(tiles)] for g in range(groups)]
    unit = [jnp.where(lane == lane0 + SUBLANES * g + sub, 1.0, 0.0).astype(jnp.float32) for g in range(groups)]
    factor_rows(rows, unit, tile, lane0, zero_ref[...])
    inside = (lane >= lane0) & (lane < lane0 + BLOCK)
    both = [[jnp.where(inside, unit[g], rows[g][t]) if t == tile else rows[g][t] for t in range(tiles)] for g in range(groups)]
    for g in range(groups):
        for t in range(tiles):
            c, r = lane + LANES * t, sub + base + SUBLANES * g
            r_ref[at(g, t)] = zeros if t < tile else rows[g][t] if t > tile else jnp.where(c >= r, rows[g][t], 0.0)
            w_ref[at(g, t)] = zeros if t > tile else rows[g][t] if t < tile else jnp.where(c <= r, both[g][t], 0.0)
    below = base + BLOCK
    if below < n:
        t0 = below // LANES
        right = jnp.concatenate([jnp.concatenate(both[g], axis=1) for g in range(groups)], axis=0)
        left = jnp.concatenate([jnp.concatenate(rows[g][t0:], axis=1) for g in range(groups)], axis=0)
        change = product(left[:, below - LANES * t0 :], right, 0, 0)
        c = lax.broadcasted_iota(jnp.int32, (n - below, n), 1)
        old = m_ref[below:, :]
        m_ref[below:, :] = jnp.where((c >= base) & (c < below), 0.0, old) - change


def factor_first_kernel(mine_ref, other_ref, m_ref, r_ref, w_ref, factor_ref, zero_ref, sem, *, stop):
    zero_ref[...] = jnp.zeros_like(zero_ref)
    unpack(mine_ref, other_ref, m_ref)
    copies = []
    for k in range(stop):
        factor_block(m_ref, r_ref, w_ref, zero_ref, k)
        if k + 1 < stop:
            at = slice(k * BLOCK, (k + 1) * BLOCK)
            copies.append(pltpu.make_async_copy(r_ref.at[at, :], factor_ref.at[at, :], sem.at[k]))
            copies[-1].start()
    for copy in copies:
        copy.wait()


def from_inverse(w_ref, x):
    half = w_ref.shape[0] // 2
    return product(w_ref[:half, :half], x[:half, :], 1, 0), product(w_ref[half:, :], x, 1, 0)


def column_half(half, mine):
    odd = lax.rem(lax.axis_index("rows"), 2)
    return pl.ds(pl.multiple_of((odd if mine else 1 - odd) * half, LANES), half)


def factor_last_kernel(
    m0_ref, r0_ref, w0_ref, panel_ref, terms_ref, trailing_ref, m_ref, r_ref, w_ref, basis_ref, c_ref, u_ref, zero_ref, *, start, stop
):
    zero_ref[...] = jnp.zeros_like(zero_ref)
    for k in range(start, stop):
        factor_block(m_ref, r_ref, w_ref, zero_ref, k)
    half = w_ref.shape[0] // 2
    basis_ref[:, :half] = product(panel_ref[:, :half], w_ref[:half, :half], 1, 1)
    basis_ref[:, half:] = product(panel_ref[...], w_ref[half:, :], 1, 1)
    coefficients = jnp.concatenate(from_inverse(w_ref, terms_ref[...]), axis=0)
    c_ref[...] = coefficients
    columns = column_half(c_ref.shape[1], True)
    u_ref[...] = trailing_ref[:, columns] - product(basis_ref[...], coefficients, 1, 0)


def cross_kernel(panel_ref, trailing_ref, keep_ref, send_ref):
    half = trailing_ref.shape[1] // 2
    terms = product(panel_ref[...], trailing_ref[...], 0, 0)
    even = lax.rem(lax.axis_index("rows"), 2) == 0

    @pl.when(even)
    def _():
        keep_ref[...] = terms[:, :half]
        send_ref[...] = terms[:, half:]

    @pl.when(jnp.logical_not(even))
    def _():
        keep_ref[...] = terms[:, half:]
        send_ref[...] = terms[:, :half]


def finish_kernel(*refs, done):
    r_ref, w_ref, basis_ref, mine_c_ref, mine_u_ref, terms_ref, trailing_ref, _, *outs, c_ref, u_ref, sems = refs
    factor_ref, coefficients_ref, updated_ref = outs
    _, wide = c_ref.shape
    mine, other = column_half(wide, True), column_half(wide, False)
    copies = []

    def send(source, target):
        copies.append(pltpu.make_async_copy(source, target, sems.at[len(copies)]))
        copies[-1].start()

    send(mine_c_ref, coefficients_ref.at[:, mine])
    send(mine_u_ref, updated_ref.at[:, mine])
    send(r_ref.at[done:, :], factor_ref.at[done:, :])
    coefficients = jnp.concatenate(from_inverse(w_ref, terms_ref[...]), axis=0)
    c_ref[...] = coefficients
    send(c_ref, coefficients_ref.at[:, other])
    tall = u_ref.shape[0] // PARTS
    for part in range(PARTS):
        at = slice(part * tall, (part + 1) * tall)
        u_ref[at, :] = trailing_ref[at, other] - product(basis_ref[at, :], coefficients, 1, 0)
        send(u_ref.at[at, :], updated_ref.at[at, other])
    for copy in copies:
        copy.wait()


def gather_steps(n_cols):
    return [*range(n_cols // 2, n_cols), *range(1, n_cols // 2)]


def local(panel, trailing, *, n_rows, n_cols):
    _, width = panel.shape
    tall, wide = trailing.shape
    half = width // 2
    bits = n_rows.bit_length() - 1
    links = bits - 1
    partner = [(i, i ^ 1) for i in range(n_rows)]
    rounds = []
    for t in range(links):
        bit = [1 + t, 1 + (t + links // 2) % links]
        rounds.append([(i, i ^ (1 << bit[i % 2])) for i in range(n_rows)])

    def sent(x, pairs, axis="rows"):
        return lax.ppermute(x, axis, pairs)

    def summed(x, pairs):
        y = sent(x, pairs)
        return x + y

    panel_here, trailing = pl.pallas_call(
        stage_kernel,
        out_shape=[pltpu.VMEM(x.shape, x.dtype) for x in (panel, trailing)],
        in_specs=[pl.BlockSpec(memory_space=pl.ANY)] * 2,
        out_specs=[pl.BlockSpec(memory_space=pltpu.VMEM)] * 2,
        scratch_shapes=[pltpu.SemaphoreType.DMA((2,))],
        name="stage",
    )(panel, trailing)
    pieces = [panel_here]
    steps = gather_steps(n_cols)
    got = {step: sent(panel, [(i, i ^ step) for i in range(n_cols)], "cols") for step in steps}
    pieces += [got[step] for step in range(1, n_cols)]
    packed, square = (half + SUBLANES, half), (width, width)
    panel_block, g, g_send = call(
        functools.partial(gram_kernel, count=n_cols), [(tall, width), packed, packed], *pieces
    )
    g = g + sent(g_send, partner)
    c, c_send = call(cross_kernel, [(width, wide // 2)] * 2, panel_block, trailing)
    c_got = sent(c_send, partner)
    c = c + c_got
    for pairs in rounds:
        g = summed(g, pairs)
    g_other = sent(g, partner)
    for pairs in rounds:
        c = summed(c, pairs)
    blocks = width // BLOCK
    zero = [pltpu.VMEM((SUBLANES, LANES), jnp.float32)]
    cuts = [blocks * 3 // 4, blocks]
    vmem, hbm = pl.BlockSpec(memory_space=pltpu.VMEM), pl.BlockSpec(memory_space=pl.ANY)
    here = lambda *xs: [pltpu.with_memory_space_constraint(x, pltpu.VMEM) for x in xs]
    inside = lambda *shapes: [pltpu.VMEM(x, jnp.float32) for x in shapes]
    results = [jax.ShapeDtypeStruct(x, jnp.float32) for x in (square, (width, wide), (tall, wide))]
    m, r, w, factor = pl.pallas_call(
        functools.partial(factor_first_kernel, stop=cuts[0]),
        out_shape=inside(square, square, square) + results[:1],
        in_specs=[vmem] * 2,
        out_specs=[vmem] * 3 + [hbm],
        scratch_shapes=zero + [pltpu.SemaphoreType.DMA((cuts[0],))],
        name="factor_first",
        compiler_params=SMALL,
    )(*here(g, g_other))
    c_other = sent(c, partner)
    _, r, w, basis, *halves = call(
        functools.partial(factor_last_kernel, start=cuts[0], stop=cuts[1]),
        [square] * 3 + [(tall, width), (width, wide // 2), (tall, wide // 2)],
        m,
        r,
        w,
        panel_block,
        c,
        trailing,
        scratch_shapes=zero,
        aliases={0: 0, 1: 1, 2: 2},
    )
    return pl.pallas_call(
        functools.partial(finish_kernel, done=(cuts[0] - 1) * BLOCK),
        out_shape=results,
        in_specs=[vmem] * 7 + [hbm],
        out_specs=[hbm] * 3,
        input_output_aliases={7: 0},
        scratch_shapes=inside((width, wide // 2), (tall, wide // 2)) + [pltpu.SemaphoreType.DMA((4 + PARTS,))],
        name="finish",
        compiler_params=SMALL,
    )(*here(r, w, basis, *halves, c_other, trailing), factor)


def solution(mesh):
    n_rows, n_cols = mesh.shape["rows"], mesh.shape["cols"]
    return jax.shard_map(
        functools.partial(local, n_rows=n_rows, n_cols=n_cols),
        mesh=mesh,
        in_specs=(P(("rows", "cols"), None), P("rows", "cols")),
        out_specs=(P(), P(None, "cols"), P("rows", "cols")),
        check_vma=False,
    )
```

```python
import functools

import jax
import jax.numpy as jnp
from jax import lax
from jax.experimental import pallas as pl
from jax.experimental.pallas import tpu as pltpu
from jax.sharding import PartitionSpec as P


LANES, SUBLANES, BLOCK, INNER, PARTS = 128, 8, 32, 4, 1

SMALL = pltpu.CompilerParams(vmem_limit_bytes=16 << 20)


def split(x):
    high = x.astype(jnp.bfloat16)
    return high, (x - high.astype(jnp.float32)).astype(jnp.bfloat16)


def product(left, right, over_left, over_right):
    lh, ll = split(left)
    rh, rl = split(right)
    return lax.dot_general(
        jnp.concatenate([lh, lh, ll], axis=over_left),
        jnp.concatenate([rh, rl, rh], axis=over_right),
        (((over_left,), (over_right,)), ((), ())),
        preferred_element_type=jnp.float32,
    )


def call(body, outs, *args, aliases=None, in_vmem=True, **extra):
    block = pl.BlockSpec(memory_space=pltpu.VMEM)
    shapes = [(pltpu.VMEM if in_vmem else jax.ShapeDtypeStruct)(s, jnp.float32) for s in outs]
    args = [pltpu.with_memory_space_constraint(x, pltpu.VMEM) for x in args]
    extra = {"in_specs": [block] * len(args), "out_specs": [block] * len(outs), "compiler_params": SMALL} | extra
    return pl.pallas_call(body, out_shape=shapes, input_output_aliases=aliases or {}, **extra)(*args)


def stage_kernel(panel_hbm, trailing_hbm, panel_ref, trailing_ref, sems):
    copies = [
        pltpu.make_async_copy(panel_hbm, panel_ref, sems.at[0]),
        pltpu.make_async_copy(trailing_hbm, trailing_ref, sems.at[1]),
    ]
    for copy in copies:
        copy.start()
    for copy in copies:
        copy.wait()


def gram_kernel(*refs, count):
    pieces, (panel_ref, keep_ref, send_ref) = refs[:count], refs[count:]
    height, width = pieces[0].shape
    half = width // 2
    here = lax.axis_index("cols")
    for step in range(count):
        at = here ^ step
        panel_ref[pl.ds(pl.multiple_of(at * height, height), height), :] = pieces[step][...]
    block = panel_ref[...]
    gram = product(block, block, 0, 0)
    row = lax.broadcasted_iota(jnp.int32, (half, half), 0)
    col = lax.broadcasted_iota(jnp.int32, (half, half), 1)
    first, cross, second = gram[:half, :half], gram[:half, half:], gram[half:, half:]
    square = jnp.where(row > col, first, second)
    spare = jnp.sum(jnp.where(row == col, first, 0.0), axis=0, keepdims=True)
    spare = jnp.broadcast_to(spare, (SUBLANES, half))
    even = lax.rem(lax.axis_index("rows"), 2) == 0

    @pl.when(even)
    def _():
        keep_ref[:half, :] = cross
        keep_ref[half:, :] = jnp.zeros((SUBLANES, half), jnp.float32)
        send_ref[:half, :] = square
        send_ref[half:, :] = spare

    @pl.when(jnp.logical_not(even))
    def _():
        send_ref[:half, :] = cross
        send_ref[half:, :] = jnp.zeros((SUBLANES, half), jnp.float32)
        keep_ref[:half, :] = square
        keep_ref[half:, :] = spare


def unpack(mine_ref, other_ref, m_ref):
    width = m_ref.shape[0]
    half = width // 2
    even = lax.rem(lax.axis_index("rows"), 2) == 0

    def place(cross_ref, square_ref):
        square = square_ref[:half, :]
        spare = square_ref[half : half + 1, :]
        row = lax.broadcasted_iota(jnp.int32, (half, half), 0)
        col = lax.broadcasted_iota(jnp.int32, (half, half), 1)
        turned = square.T
        m_ref[:half, :half] = jnp.where(row > col, square, jnp.where(row < col, turned, spare))
        m_ref[half:, half:] = jnp.where(row <= col, square, turned)
        m_ref[:half, half:] = cross_ref[:half, :]
        m_ref[half:, :half] = jnp.zeros((half, half), jnp.float32)

    pl.when(even)(functools.partial(place, mine_ref, other_ref))
    pl.when(jnp.logical_not(even))(functools.partial(place, other_ref, mine_ref))


def along_sublanes(x, r):
    return jnp.broadcast_to(x[r : r + 1, :], x.shape)


def along_lanes(x, c):
    return jnp.broadcast_to(x[:, c : c + 1], (x.shape[0], LANES))


def factor_rows(rows, unit, tile, lane0, zero):
    groups, tiles = len(rows), len(rows[0])
    sub = lax.broadcasted_iota(jnp.int32, (SUBLANES, LANES), 0)
    for j in range(groups):
        own = rows[j] + [unit[j]]
        spread = lambda step: {
            g: [along_lanes(rows[g][tile], lane0 + SUBLANES * step + c) for c in range(SUBLANES)]
            for g in range(step, groups)
        }
        if j == 0:
            col = spread(0)
            col[0] = [x - zero for x in col[0]]
        else:
            col = following
        following = spread(j + 1)
        head = list(col[j])
        low, ours, done, scales = {}, [], [], zero
        for i in range(SUBLANES):
            start = i - i % INNER
            stop = start + INNER
            if i == start:
                for c in range(i, SUBLANES):
                    for m in range(max(start - INNER, 0), start):
                        low[c, m] = along_sublanes(ours[m], c)
                        head[c] = head[c] - ours[m] * low[c, m]
                pivot = {(r, c): along_sublanes(head[c], r) for c in range(i, stop) for r in range(c, stop)}
            scale = lax.rsqrt(pivot[i, i])
            scales = jnp.where(sub == i, scale, scales)
            for r in range(i + 1, stop):
                low[r, i] = pivot[r, i] * scale
            for c in range(i + 1, stop):
                for r in range(c, stop):
                    pivot[r, c] = pivot[r, c] - low[r, i] * low[c, i]
            x = head[i]
            for m in range(start, i):
                x = x - ours[m] * low[i, m]
            ours.append(x * scale)
            done.append([along_sublanes(x, i) * scale for x in own])
            if i + 1 < SUBLANES:
                below = jnp.where(sub > i, ours[i], zero)
                own = [x - below * y for x, y in zip(own, done[i])]
            for g in range(j + 1, groups):
                x = col[g][i]
                for m in range(i):
                    x = x - col[g][m] * low[i, m]
                col[g][i] = x * scale
            for c in range(SUBLANES if j + 1 < groups else 0):
                factor = along_sublanes(col[j + 1][i], c)
                for g in range(j + 1, groups):
                    following[g][c] = following[g][c] - col[g][i] * factor
        own = [x * scales for x in own]
        rows[j], unit[j] = own[:tiles], own[tiles]
        for g in range(j + 1, groups):
            for i in range(SUBLANES):
                for t in range(tiles):
                    rows[g][t] = rows[g][t] - col[g][i] * done[i][t]
                unit[g] = unit[g] - col[g][i] * done[i][tiles]


def factor_block(m_ref, r_ref, w_ref, zero_ref, k):
    n = m_ref.shape[0]
    tiles, groups = n // LANES, BLOCK // SUBLANES
    sub = lax.broadcasted_iota(jnp.int32, (SUBLANES, LANES), 0)
    lane = lax.broadcasted_iota(jnp.int32, (SUBLANES, LANES), 1)
    zeros = jnp.zeros((SUBLANES, LANES), jnp.float32)
    base = k * BLOCK
    tile, lane0 = base // LANES, base % LANES
    at = lambda g, t: (slice(base + SUBLANES * g, base + SUBLANES * (g + 1)), slice(LANES * t, LANES * (t + 1)))
    rows = [[m_ref[at(g, t)] for t in range(tiles)] for g in range(groups)]
    unit = [jnp.where(lane == lane0 + SUBLANES * g + sub, 1.0, 0.0).astype(jnp.float32) for g in range(groups)]
    factor_rows(rows, unit, tile, lane0, zero_ref[...])
    inside = (lane >= lane0) & (lane < lane0 + BLOCK)
    both = [[jnp.where(inside, unit[g], rows[g][t]) if t == tile else rows[g][t] for t in range(tiles)] for g in range(groups)]
    for g in range(groups):
        for t in range(tiles):
            c, r = lane + LANES * t, sub + base + SUBLANES * g
            r_ref[at(g, t)] = zeros if t < tile else rows[g][t] if t > tile else jnp.where(c >= r, rows[g][t], 0.0)
            w_ref[at(g, t)] = zeros if t > tile else rows[g][t] if t < tile else jnp.where(c <= r, both[g][t], 0.0)
    below = base + BLOCK
    if below < n:
        t0 = below // LANES
        right = jnp.concatenate([jnp.concatenate(both[g], axis=1) for g in range(groups)], axis=0)
        left = jnp.concatenate([jnp.concatenate(rows[g][t0:], axis=1) for g in range(groups)], axis=0)
        change = product(left[:, below - LANES * t0 :], right, 0, 0)
        c = lax.broadcasted_iota(jnp.int32, (n - below, n), 1)
        old = m_ref[below:, :]
        m_ref[below:, :] = jnp.where((c >= base) & (c < below), 0.0, old) - change


def factor_first_kernel(
    mine_ref, other_ref, panel_ref, m_ref, r_ref, w_ref, basis_ref, factor_ref, zero_ref, sem, *, stop
):
    zero_ref[...] = jnp.zeros_like(zero_ref)
    unpack(mine_ref, other_ref, m_ref)
    copies = []
    for k in range(stop):
        factor_block(m_ref, r_ref, w_ref, zero_ref, k)
        if k + 1 < stop:
            at = slice(k * BLOCK, (k + 1) * BLOCK)
            copies.append(pltpu.make_async_copy(r_ref.at[at, :], factor_ref.at[at, :], sem.at[k]))
            copies[-1].start()
    half = w_ref.shape[0] // 2
    basis_ref[...] = product(panel_ref[:, :half], w_ref[:half, :half], 1, 1)
    for copy in copies:
        copy.wait()


def from_inverse(w_ref, x):
    half = w_ref.shape[0] // 2
    return product(w_ref[:half, :half], x[:half, :], 1, 0), product(w_ref[half:, :], x, 1, 0)


def column_half(half, mine):
    odd = lax.rem(lax.axis_index("rows"), 2)
    return pl.ds(pl.multiple_of((odd if mine else 1 - odd) * half, LANES), half)


def factor_last_kernel(
    m0_ref, r0_ref, w0_ref, basis0_ref, panel_ref, terms_ref, trailing_ref, m_ref, r_ref, w_ref, basis_ref, c_ref, u_ref, zero_ref, *, start, stop
):
    zero_ref[...] = jnp.zeros_like(zero_ref)
    for k in range(start, stop):
        factor_block(m_ref, r_ref, w_ref, zero_ref, k)
    half = w_ref.shape[0] // 2
    basis_ref[:, :half] = basis0_ref[...]
    basis_ref[:, half:] = product(panel_ref[...], w_ref[half:, :], 1, 1)
    coefficients = jnp.concatenate(from_inverse(w_ref, terms_ref[...]), axis=0)
    c_ref[...] = coefficients
    columns = column_half(c_ref.shape[1], True)
    u_ref[...] = trailing_ref[:, columns] - product(basis_ref[...], coefficients, 1, 0)


def cross_kernel(panel_ref, trailing_ref, keep_ref, send_ref):
    half = trailing_ref.shape[1] // 2
    terms = product(panel_ref[...], trailing_ref[...], 0, 0)
    even = lax.rem(lax.axis_index("rows"), 2) == 0

    @pl.when(even)
    def _():
        keep_ref[...] = terms[:, :half]
        send_ref[...] = terms[:, half:]

    @pl.when(jnp.logical_not(even))
    def _():
        keep_ref[...] = terms[:, half:]
        send_ref[...] = terms[:, :half]


def finish_kernel(*refs, done):
    r_ref, w_ref, basis_ref, mine_c_ref, mine_u_ref, terms_ref, trailing_ref, _, *outs, c_ref, u_ref, sems = refs
    factor_ref, coefficients_ref, updated_ref = outs
    _, wide = c_ref.shape
    mine, other = column_half(wide, True), column_half(wide, False)
    copies = []

    def send(source, target):
        copies.append(pltpu.make_async_copy(source, target, sems.at[len(copies)]))
        copies[-1].start()

    send(mine_c_ref, coefficients_ref.at[:, mine])
    send(mine_u_ref, updated_ref.at[:, mine])
    send(r_ref.at[done:, :], factor_ref.at[done:, :])
    coefficients = jnp.concatenate(from_inverse(w_ref, terms_ref[...]), axis=0)
    c_ref[...] = coefficients
    send(c_ref, coefficients_ref.at[:, other])
    tall = u_ref.shape[0] // PARTS
    for part in range(PARTS):
        at = slice(part * tall, (part + 1) * tall)
        u_ref[at, :] = trailing_ref[at, other] - product(basis_ref[at, :], coefficients, 1, 0)
        send(u_ref.at[at, :], updated_ref.at[at, other])
    for copy in copies:
        copy.wait()


def gather_steps(n_cols):
    return [*range(n_cols // 2, n_cols), *range(1, n_cols // 2)]


def local(panel, trailing, *, n_rows, n_cols):
    _, width = panel.shape
    tall, wide = trailing.shape
    half = width // 2
    bits = n_rows.bit_length() - 1
    links = bits - 1
    partner = [(i, i ^ 1) for i in range(n_rows)]
    rounds = []
    for t in range(links):
        bit = [1 + t, 1 + (t + links // 2) % links]
        rounds.append([(i, i ^ (1 << bit[i % 2])) for i in range(n_rows)])

    def sent(x, pairs, axis="rows"):
        return lax.ppermute(x, axis, pairs)

    def summed(x, pairs):
        y = sent(x, pairs)
        return x + y

    panel_here, trailing = pl.pallas_call(
        stage_kernel,
        out_shape=[pltpu.VMEM(x.shape, x.dtype) for x in (panel, trailing)],
        in_specs=[pl.BlockSpec(memory_space=pl.ANY)] * 2,
        out_specs=[pl.BlockSpec(memory_space=pltpu.VMEM)] * 2,
        scratch_shapes=[pltpu.SemaphoreType.DMA((2,))],
        name="stage",
    )(panel, trailing)
    pieces = [panel_here]
    steps = gather_steps(n_cols)
    got = {step: sent(panel, [(i, i ^ step) for i in range(n_cols)], "cols") for step in steps}
    pieces += [got[step] for step in range(1, n_cols)]
    packed, square = (half + SUBLANES, half), (width, width)
    panel_block, g, g_send = call(
        functools.partial(gram_kernel, count=n_cols), [(tall, width), packed, packed], *pieces
    )
    g = g + sent(g_send, partner)
    c, c_send = call(cross_kernel, [(width, wide // 2)] * 2, panel_block, trailing)
    c_got = sent(c_send, partner)
    c = c + c_got
    for pairs in rounds:
        g = summed(g, pairs)
    g_other = sent(g, partner)
    for pairs in rounds:
        c = summed(c, pairs)
    blocks = width // BLOCK
    zero = [pltpu.VMEM((SUBLANES, LANES), jnp.float32)]
    cuts = [blocks * 3 // 4, blocks]
    vmem, hbm = pl.BlockSpec(memory_space=pltpu.VMEM), pl.BlockSpec(memory_space=pl.ANY)
    here = lambda *xs: [pltpu.with_memory_space_constraint(x, pltpu.VMEM) for x in xs]
    inside = lambda *shapes: [pltpu.VMEM(x, jnp.float32) for x in shapes]
    results = [jax.ShapeDtypeStruct(x, jnp.float32) for x in (square, (width, wide), (tall, wide))]
    m, r, w, basis, factor = pl.pallas_call(
        functools.partial(factor_first_kernel, stop=cuts[0]),
        out_shape=inside(square, square, square, (tall, half)) + results[:1],
        in_specs=[vmem] * 3,
        out_specs=[vmem] * 4 + [hbm],
        scratch_shapes=zero + [pltpu.SemaphoreType.DMA((cuts[0],))],
        name="factor_first",
        compiler_params=SMALL,
    )(*here(g, g_other, panel_block))
    c_other = sent(c, partner)
    _, r, w, basis, *halves = call(
        functools.partial(factor_last_kernel, start=cuts[0], stop=cuts[1]),
        [square] * 3 + [(tall, width), (width, wide // 2), (tall, wide // 2)],
        m,
        r,
        w,
        basis,
        panel_block,
        c,
        trailing,
        scratch_shapes=zero,
        aliases={0: 0, 1: 1, 2: 2},
    )
    return pl.pallas_call(
        functools.partial(finish_kernel, done=(cuts[0] - 1) * BLOCK),
        out_shape=results,
        in_specs=[vmem] * 7 + [hbm],
        out_specs=[hbm] * 3,
        input_output_aliases={7: 0},
        scratch_shapes=inside((width, wide // 2), (tall, wide // 2)) + [pltpu.SemaphoreType.DMA((4 + PARTS,))],
        name="finish",
        compiler_params=SMALL,
    )(*here(r, w, basis, *halves, c_other, trailing), factor)


def solution(mesh):
    n_rows, n_cols = mesh.shape["rows"], mesh.shape["cols"]
    return jax.shard_map(
        functools.partial(local, n_rows=n_rows, n_cols=n_cols),
        mesh=mesh,
        in_specs=(P(("rows", "cols"), None), P("rows", "cols")),
        out_specs=(P(), P(None, "cols"), P("rows", "cols")),
        check_vma=False,
    )
```

```python
import functools

import jax
import jax.numpy as jnp
from jax import lax
from jax.experimental import pallas as pl
from jax.experimental.pallas import tpu as pltpu
from jax.sharding import PartitionSpec as P


LANES, SUBLANES, BLOCK, INNER, PARTS = 128, 8, 32, 4, 1

SMALL = pltpu.CompilerParams(vmem_limit_bytes=16 << 20)


def split(x):
    high = x.astype(jnp.bfloat16)
    return high, (x - high.astype(jnp.float32)).astype(jnp.bfloat16)


def product(left, right, over_left, over_right):
    lh, ll = split(left)
    rh, rl = split(right)
    return lax.dot_general(
        jnp.concatenate([lh, lh, ll], axis=over_left),
        jnp.concatenate([rh, rl, rh], axis=over_right),
        (((over_left,), (over_right,)), ((), ())),
        preferred_element_type=jnp.float32,
    )


def call(body, outs, *args, aliases=None, **extra):
    block = pl.BlockSpec(memory_space=pltpu.VMEM)
    shapes = [pltpu.VMEM(s, jnp.float32) if isinstance(s, tuple) else s for s in outs]
    args = [pltpu.with_memory_space_constraint(x, pltpu.VMEM) for x in args]
    extra = {"in_specs": [block] * len(args), "out_specs": [block] * len(outs), "compiler_params": SMALL} | extra
    return pl.pallas_call(body, out_shape=shapes, input_output_aliases=aliases or {}, **extra)(*args)


def stage_kernel(panel_hbm, trailing_hbm, panel_ref, trailing_ref, sems):
    copies = [
        pltpu.make_async_copy(panel_hbm, panel_ref, sems.at[0]),
        pltpu.make_async_copy(trailing_hbm, trailing_ref, sems.at[1]),
    ]
    for copy in copies:
        copy.start()
    for copy in copies:
        copy.wait()


def gram_kernel(*refs, count):
    pieces, (panel_ref, keep_ref, send_ref) = refs[:count], refs[count:]
    height, width = pieces[0].shape
    half = width // 2
    here = lax.axis_index("cols")
    for step in range(count):
        at = here ^ step
        panel_ref[pl.ds(pl.multiple_of(at * height, height), height), :] = pieces[step][...]
    block = panel_ref[...]
    gram = product(block, block, 0, 0)
    row = lax.broadcasted_iota(jnp.int32, (half, half), 0)
    col = lax.broadcasted_iota(jnp.int32, (half, half), 1)
    first, cross, second = gram[:half, :half], gram[:half, half:], gram[half:, half:]
    square = jnp.where(row > col, first, second)
    spare = jnp.sum(jnp.where(row == col, first, 0.0), axis=0, keepdims=True)
    spare = jnp.broadcast_to(spare, (SUBLANES, half))
    even = lax.rem(lax.axis_index("rows"), 2) == 0

    @pl.when(even)
    def _():
        keep_ref[:half, :] = cross
        keep_ref[half:, :] = jnp.zeros((SUBLANES, half), jnp.float32)
        send_ref[:half, :] = square
        send_ref[half:, :] = spare

    @pl.when(jnp.logical_not(even))
    def _():
        send_ref[:half, :] = cross
        send_ref[half:, :] = jnp.zeros((SUBLANES, half), jnp.float32)
        keep_ref[:half, :] = square
        keep_ref[half:, :] = spare


def unpack(mine_ref, other_ref, m_ref):
    width = m_ref.shape[0]
    half = width // 2
    even = lax.rem(lax.axis_index("rows"), 2) == 0

    def place(cross_ref, square_ref):
        square = square_ref[:half, :]
        spare = square_ref[half : half + 1, :]
        row = lax.broadcasted_iota(jnp.int32, (half, half), 0)
        col = lax.broadcasted_iota(jnp.int32, (half, half), 1)
        turned = square.T
        m_ref[:half, :half] = jnp.where(row > col, square, jnp.where(row < col, turned, spare))
        m_ref[half:, half:] = jnp.where(row <= col, square, turned)
        m_ref[:half, half:] = cross_ref[:half, :]
        m_ref[half:, :half] = jnp.zeros((half, half), jnp.float32)

    pl.when(even)(functools.partial(place, mine_ref, other_ref))
    pl.when(jnp.logical_not(even))(functools.partial(place, other_ref, mine_ref))


def along_sublanes(x, r):
    return jnp.broadcast_to(x[r : r + 1, :], x.shape)


def along_lanes(x, c):
    return jnp.broadcast_to(x[:, c : c + 1], (x.shape[0], LANES))


def factor_rows(rows, unit, tile, lane0, zero):
    groups, tiles = len(rows), len(rows[0])
    sub = lax.broadcasted_iota(jnp.int32, (SUBLANES, LANES), 0)
    for j in range(groups):
        own = rows[j] + [unit[j]]
        spread = lambda step: {
            g: [along_lanes(rows[g][tile], lane0 + SUBLANES * step + c) for c in range(SUBLANES)]
            for g in range(step, groups)
        }
        if j == 0:
            col = spread(0)
            col[0] = [x - zero for x in col[0]]
        else:
            col = following
        following = spread(j + 1)
        head = list(col[j])
        low, ours, done, scales = {}, [], [], zero
        for i in range(SUBLANES):
            start = i - i % INNER
            stop = start + INNER
            if i == start:
                for c in range(i, SUBLANES):
                    for m in range(max(start - INNER, 0), start):
                        low[c, m] = along_sublanes(ours[m], c)
                        head[c] = head[c] - ours[m] * low[c, m]
                pivot = {(r, c): along_sublanes(head[c], r) for c in range(i, stop) for r in range(c, stop)}
            scale = lax.rsqrt(pivot[i, i])
            scales = jnp.where(sub == i, scale, scales)
            for r in range(i + 1, stop):
                low[r, i] = pivot[r, i] * scale
            for c in range(i + 1, stop):
                for r in range(c, stop):
                    pivot[r, c] = pivot[r, c] - low[r, i] * low[c, i]
            x = head[i]
            for m in range(start, i):
                x = x - ours[m] * low[i, m]
            ours.append(x * scale)
            done.append([along_sublanes(x, i) * scale for x in own])
            if i + 1 < SUBLANES:
                below = jnp.where(sub > i, ours[i], zero)
                own = [x - below * y for x, y in zip(own, done[i])]
            for g in range(j + 1, groups):
                x = col[g][i]
                for m in range(i):
                    x = x - col[g][m] * low[i, m]
                col[g][i] = x * scale
            for c in range(SUBLANES if j + 1 < groups else 0):
                factor = along_sublanes(col[j + 1][i], c)
                for g in range(j + 1, groups):
                    following[g][c] = following[g][c] - col[g][i] * factor
        own = [x * scales for x in own]
        rows[j], unit[j] = own[:tiles], own[tiles]
        for g in range(j + 1, groups):
            for i in range(SUBLANES):
                for t in range(tiles):
                    rows[g][t] = rows[g][t] - col[g][i] * done[i][t]
                unit[g] = unit[g] - col[g][i] * done[i][tiles]


def factor_block(m_ref, r_ref, w_ref, zero_ref, k):
    n = m_ref.shape[0]
    tiles, groups = n // LANES, BLOCK // SUBLANES
    sub = lax.broadcasted_iota(jnp.int32, (SUBLANES, LANES), 0)
    lane = lax.broadcasted_iota(jnp.int32, (SUBLANES, LANES), 1)
    zeros = jnp.zeros((SUBLANES, LANES), jnp.float32)
    base = k * BLOCK
    tile, lane0 = base // LANES, base % LANES
    at = lambda g, t: (slice(base + SUBLANES * g, base + SUBLANES * (g + 1)), slice(LANES * t, LANES * (t + 1)))
    rows = [[m_ref[at(g, t)] for t in range(tiles)] for g in range(groups)]
    unit = [jnp.where(lane == lane0 + SUBLANES * g + sub, 1.0, 0.0).astype(jnp.float32) for g in range(groups)]
    factor_rows(rows, unit, tile, lane0, zero_ref[...])
    inside = (lane >= lane0) & (lane < lane0 + BLOCK)
    both = [[jnp.where(inside, unit[g], rows[g][t]) if t == tile else rows[g][t] for t in range(tiles)] for g in range(groups)]
    for g in range(groups):
        for t in range(tiles):
            c, r = lane + LANES * t, sub + base + SUBLANES * g
            r_ref[at(g, t)] = zeros if t < tile else rows[g][t] if t > tile else jnp.where(c >= r, rows[g][t], 0.0)
            w_ref[at(g, t)] = zeros if t > tile else rows[g][t] if t < tile else jnp.where(c <= r, both[g][t], 0.0)
    below = base + BLOCK
    if below < n:
        t0 = below // LANES
        right = jnp.concatenate([jnp.concatenate(both[g], axis=1) for g in range(groups)], axis=0)
        left = jnp.concatenate([jnp.concatenate(rows[g][t0:], axis=1) for g in range(groups)], axis=0)
        change = product(left[:, below - LANES * t0 :], right, 0, 0)
        c = lax.broadcasted_iota(jnp.int32, (n - below, n), 1)
        old = m_ref[below:, :]
        m_ref[below:, :] = jnp.where((c >= base) & (c < below), 0.0, old) - change


def factor_first_kernel(
    mine_ref, other_ref, panel_ref, m_ref, r_ref, w_ref, basis_ref, factor_ref, zero_ref, sem, *, stop
):
    zero_ref[...] = jnp.zeros_like(zero_ref)
    unpack(mine_ref, other_ref, m_ref)
    copies = []
    for k in range(stop):
        factor_block(m_ref, r_ref, w_ref, zero_ref, k)
        if k + 1 < stop:
            at = slice(k * BLOCK, (k + 1) * BLOCK)
            copies.append(pltpu.make_async_copy(r_ref.at[at, :], factor_ref.at[at, :], sem.at[k]))
            copies[-1].start()
    half = w_ref.shape[0] // 2
    basis_ref[...] = product(panel_ref[:, :half], w_ref[:half, :half], 1, 1)
    for copy in copies:
        copy.wait()


def stack(x):
    high, low = split(x)
    return jnp.concatenate([high, high, low], axis=1)


def stacked_product(stacked, right):
    high, low = split(right)
    return jnp.dot(stacked, jnp.concatenate([high, low, high], axis=0), preferred_element_type=jnp.float32)


def from_inverse(top, low, x):
    return stacked_product(top, x[: x.shape[0] // 2, :]), stacked_product(low, x)


def column_half(half, mine):
    odd = lax.rem(lax.axis_index("rows"), 2)
    return pl.ds(pl.multiple_of((odd if mine else 1 - odd) * half, LANES), half)


def factor_last_kernel(
    m0_ref, r0_ref, w0_ref, basis0_ref, panel_ref, terms_ref, trailing_ref, m_ref, r_ref, w_ref, top_ref, low_ref, basis_ref, c_ref, u_ref, zero_ref, *, start, stop
):
    zero_ref[...] = jnp.zeros_like(zero_ref)
    for k in range(start, stop):
        factor_block(m_ref, r_ref, w_ref, zero_ref, k)
    half = w_ref.shape[0] // 2
    rest = product(panel_ref[...], w_ref[half:, :], 1, 1)
    basis_ref[...] = stack(jnp.concatenate([basis0_ref[...], rest], axis=1))
    top_ref[...] = stack(w_ref[:half, :half])
    low_ref[...] = stack(w_ref[half:, :])
    coefficients = jnp.concatenate(from_inverse(top_ref[...], low_ref[...], terms_ref[...]), axis=0)
    c_ref[...] = coefficients
    columns = column_half(c_ref.shape[1], True)
    u_ref[...] = trailing_ref[:, columns] - stacked_product(basis_ref[...], coefficients)


def cross_kernel(panel_ref, trailing_ref, keep_ref, send_ref):
    half = trailing_ref.shape[1] // 2
    terms = product(panel_ref[...], trailing_ref[...], 0, 0)
    even = lax.rem(lax.axis_index("rows"), 2) == 0

    @pl.when(even)
    def _():
        keep_ref[...] = terms[:, :half]
        send_ref[...] = terms[:, half:]

    @pl.when(jnp.logical_not(even))
    def _():
        keep_ref[...] = terms[:, half:]
        send_ref[...] = terms[:, :half]


def finish_kernel(*refs, done):
    r_ref, top_ref, low_ref, basis_ref, mine_c_ref, mine_u_ref, terms_ref, trailing_ref, _, *outs, c_ref, u_ref, sems = refs
    factor_ref, coefficients_ref, updated_ref = outs
    _, wide = c_ref.shape
    mine, other = column_half(wide, True), column_half(wide, False)
    copies = []

    def send(source, target):
        copies.append(pltpu.make_async_copy(source, target, sems.at[len(copies)]))
        copies[-1].start()

    send(mine_c_ref, coefficients_ref.at[:, mine])
    send(mine_u_ref, updated_ref.at[:, mine])
    send(r_ref.at[done:, :], factor_ref.at[done:, :])
    coefficients = jnp.concatenate(from_inverse(top_ref[...], low_ref[...], terms_ref[...]), axis=0)
    c_ref[...] = coefficients
    send(c_ref, coefficients_ref.at[:, other])
    tall = u_ref.shape[0] // PARTS
    for part in range(PARTS):
        at = slice(part * tall, (part + 1) * tall)
        u_ref[at, :] = trailing_ref[at, other] - stacked_product(basis_ref[at, :], coefficients)
        send(u_ref.at[at, :], updated_ref.at[at, other])
    for copy in copies:
        copy.wait()


def gather_steps(n_cols):
    return [*range(n_cols // 2, n_cols), *range(1, n_cols // 2)]


def local(panel, trailing, *, n_rows, n_cols):
    _, width = panel.shape
    tall, wide = trailing.shape
    half = width // 2
    bits = n_rows.bit_length() - 1
    links = bits - 1
    partner = [(i, i ^ 1) for i in range(n_rows)]
    rounds = []
    for t in range(links):
        bit = [1 + t, 1 + (t + links // 2) % links]
        rounds.append([(i, i ^ (1 << bit[i % 2])) for i in range(n_rows)])

    def sent(x, pairs, axis="rows"):
        return lax.ppermute(x, axis, pairs)

    def summed(x, pairs):
        y = sent(x, pairs)
        return x + y

    panel_here, trailing = pl.pallas_call(
        stage_kernel,
        out_shape=[pltpu.VMEM(x.shape, x.dtype) for x in (panel, trailing)],
        in_specs=[pl.BlockSpec(memory_space=pl.ANY)] * 2,
        out_specs=[pl.BlockSpec(memory_space=pltpu.VMEM)] * 2,
        scratch_shapes=[pltpu.SemaphoreType.DMA((2,))],
        name="stage",
    )(panel, trailing)
    pieces = [panel_here]
    steps = gather_steps(n_cols)
    got = {step: sent(panel, [(i, i ^ step) for i in range(n_cols)], "cols") for step in steps}
    pieces += [got[step] for step in range(1, n_cols)]
    packed, square = (half + SUBLANES, half), (width, width)
    panel_block, g, g_send = call(
        functools.partial(gram_kernel, count=n_cols), [(tall, width), packed, packed], *pieces
    )
    g = g + sent(g_send, partner)
    c, c_send = call(cross_kernel, [(width, wide // 2)] * 2, panel_block, trailing)
    c_got = sent(c_send, partner)
    c = c + c_got
    for pairs in rounds:
        g = summed(g, pairs)
    g_other = sent(g, partner)
    for pairs in rounds:
        c = summed(c, pairs)
    blocks = width // BLOCK
    zero = [pltpu.VMEM((SUBLANES, LANES), jnp.float32)]
    cuts = [blocks * 7 // 8, blocks]
    vmem, hbm = pl.BlockSpec(memory_space=pltpu.VMEM), pl.BlockSpec(memory_space=pl.ANY)
    here = lambda *xs: [pltpu.with_memory_space_constraint(x, pltpu.VMEM) for x in xs]
    inside = lambda *shapes: [pltpu.VMEM(x, jnp.float32) for x in shapes]
    results = [jax.ShapeDtypeStruct(x, jnp.float32) for x in (square, (width, wide), (tall, wide))]
    m, r, w, basis, factor = pl.pallas_call(
        functools.partial(factor_first_kernel, stop=cuts[0]),
        out_shape=inside(square, square, square, (tall, half)) + results[:1],
        in_specs=[vmem] * 3,
        out_specs=[vmem] * 4 + [hbm],
        scratch_shapes=zero + [pltpu.SemaphoreType.DMA((cuts[0],))],
        name="factor_first",
        compiler_params=SMALL,
    )(*here(g, g_other, panel_block))
    c_other = sent(c, partner)
    stacks = [pltpu.VMEM(x, jnp.bfloat16) for x in ((half, 3 * half), (half, 3 * width), (tall, 3 * width))]
    _, r, _, top, low, basis, *halves = call(
        functools.partial(factor_last_kernel, start=cuts[0], stop=cuts[1]),
        [square] * 3 + stacks + [(width, wide // 2), (tall, wide // 2)],
        m,
        r,
        w,
        basis,
        panel_block,
        c,
        trailing,
        scratch_shapes=zero,
        aliases={0: 0, 1: 1, 2: 2},
    )
    return pl.pallas_call(
        functools.partial(finish_kernel, done=(cuts[0] - 1) * BLOCK),
        out_shape=results,
        in_specs=[vmem] * 8 + [hbm],
        out_specs=[hbm] * 3,
        input_output_aliases={8: 0},
        scratch_shapes=inside((width, wide // 2), (tall, wide // 2)) + [pltpu.SemaphoreType.DMA((4 + PARTS,))],
        name="finish",
        compiler_params=SMALL,
    )(*here(r, top, low, basis, *halves, c_other, trailing), factor)


def solution(mesh):
    n_rows, n_cols = mesh.shape["rows"], mesh.shape["cols"]
    return jax.shard_map(
        functools.partial(local, n_rows=n_rows, n_cols=n_cols),
        mesh=mesh,
        in_specs=(P(("rows", "cols"), None), P("rows", "cols")),
        out_specs=(P(), P(None, "cols"), P("rows", "cols")),
        check_vma=False,
    )
```
